32 devices in a mesh: dp: 8 (over z, x), tensor: 4 (over y, core).
Axes of the slice: x: 2, y: 2, z: 4, core: 2. Of those that a mesh axis runs over, the one named last changes fastest.
Arguments:
- tokens: bfloat16 [4096, 4096], P(('dp', 'tensor')), may hold values from -6 to 6
- norm_gain: float32 [4096], replicated, may hold values from 0.1 to 1.9
- w_query: bfloat16 [4096, 2048], P(None, 'tensor'), may hold values from -2 to 2
- key_weight: bfloat16 [4096, 512], P(None, 'tensor'), may hold values from -0.09375 to 0.09375
- value_weight: bfloat16 [4096, 512], P(None, 'tensor'), may hold values from -0.09375 to 0.09375
- w_out: bfloat16 [2048, 4096], P('tensor'), may hold values from -0.125 to 0.125
- lengths: int32 [4], replicated, may hold values from 1 to 2560, 4096 in all
Outputs:
- layer_out: bfloat16 [4096, 4096], P(('dp', 'tensor'))
The draws below stay inside these ranges and needn't reach their ends.
Inputs may be any that keep to these rules, and one draw needn't show every extreme that they name: The lengths sum to 4096, and some document has exactly 2560 tokens.
All inputs are finite; a program needn't handle non-finite values.
Results may differ from the reference program's by a relative error of at most 0.0095.
The reference program's roundings to bfloat16 on the way count: a program that leaves them out, or rounds other values in their place, can miss the bound.
Values may be sent and summed in bfloat16 or wider, within the bound.
A program may use at most 128 MiB of HBM per device.

```python
import math
import jax
import jax.numpy as jnp
import numpy as np
from jax import lax

MODEL_WIDTH = 4096
QUERY_HEADS = 16
KEY_VALUE_HEADS = 4
HEAD_SIZE = 128
DOC_MAX = 2560
TOKENS = 4096
NDOC = 4


def draw_w_query(key, part):
    folded = jax.random.fold_in(key, 7331)
    base_key, selection_key, magnitude_key = jax.random.split(folded, 3)
    width = QUERY_HEADS * HEAD_SIZE
    base = jax.random.normal(base_key, (MODEL_WIDTH, width), jnp.float32)
    group_count = QUERY_HEADS // KEY_VALUE_HEADS
    selected = jax.random.randint(selection_key, (KEY_VALUE_HEADS,), 0, group_count)
    magnitude = jnp.exp(jax.random.uniform(magnitude_key, (KEY_VALUE_HEADS,), jnp.float32, math.log(30.0), math.log(60.0)))
    head_index = jnp.arange(QUERY_HEADS, dtype=jnp.int32)
    owner = head_index // group_count
    strong = head_index % group_count == selected[owner]
    factor = jnp.where(strong, magnitude[owner], 1.0)
    columns = jnp.repeat(factor, HEAD_SIZE)
    scaled = base * MODEL_WIDTH ** (-0.5) * columns[None, :]
    return jnp.clip(scaled, -2.0, 2.0).astype(jnp.bfloat16)


def block_scale(own_key, shape, cuts, least, largest):
    factor_of, own = 1.0, jax.random.fold_in(own_key, 6)
    for position, shards_of in cuts:
        steps = jnp.exp(jax.random.uniform(jax.random.fold_in(own, position), (shards_of,), jnp.float32, least / len(cuts), largest / len(cuts)))
        factor_of = factor_of * jnp.repeat(steps, shape[position] // shards_of).reshape([-1 if axis == position else 1 for axis in range(len(shape))])
    return factor_of


def profile(number_of, total, limit, lean):
    weights = [(1 << 20) // math.isqrt(rank ** lean) + 1 for rank in range(2, number_of + 1)]
    surplus, counts = total - limit - (number_of - 1), [1] * (number_of - 1)
    while surplus > 0:
        free = [i for i in range(number_of - 1) if counts[i] < limit]
        whole, remaining = sum([weights[i] for i in free]), surplus
        for i in free:
            extra = min(limit - counts[i], max(1, remaining * weights[i] // whole), surplus)
            counts[i] = counts[i] + extra
            surplus = surplus - extra
    return np.array([limit] + counts)


def uneven_parts(key, count, total, reach, skew):
    if count == 2:
        one = jax.random.randint(key, (), max(1, total - reach), min(reach, total - 1) + 1)
        return jnp.stack([one, total - one])
    sizes = jnp.asarray(profile(count, total, reach, skew), jnp.int32)
    pairs = (count - 1) // 2
    giver, receiver = sizes[1:1 + 2 * pairs:2], sizes[2:2 + 2 * pairs:2]
    slack = jnp.minimum(giver - 1, reach - receiver)
    shifted = jax.random.randint(jax.random.fold_in(key, 1), (pairs,), 0, 1 << 20) % (slack + 1)
    sizes = sizes.at[1:1 + 2 * pairs:2].set(giver - shifted).at[2:2 + 2 * pairs:2].set(receiver + shifted)
    return sizes[jax.random.permutation(jax.random.fold_in(key, 2), count)]


def centred(own_key, extent, spread, bound, cuts=(), kind=jnp.bfloat16):
    factor_of = block_scale(own_key, extent, cuts, -0.22, 0.18) if cuts else 1.0
    entries = jax.random.normal(own_key, extent, jnp.float32) * spread * factor_of
    return jnp.minimum(jnp.maximum(entries, -bound), bound).astype(kind)


def setup_inputs(seed: int = 0) -> dict:
    key_list = jax.random.split(jax.random.key(seed), 8)
    tokens = centred(key_list[0], (TOKENS, MODEL_WIDTH), 1.0, 6.0, ((0, 32),))
    norm_gain = jnp.clip(1.0 + 0.18 * jax.random.normal(key_list[1], (MODEL_WIDTH,), jnp.float32), 0.1, 1.9)
    w_query = draw_w_query(jax.random.fold_in(key_list[7], 71), 0)
    key_weight = centred(key_list[3], (MODEL_WIDTH, KEY_VALUE_HEADS * HEAD_SIZE), MODEL_WIDTH ** -0.5, 0.09375, ((1, 4),))
    value_weight = centred(key_list[4], (MODEL_WIDTH, KEY_VALUE_HEADS * HEAD_SIZE), MODEL_WIDTH ** -0.5, 0.09375, ((1, 4),))
    w_out = centred(key_list[5], (QUERY_HEADS * HEAD_SIZE, MODEL_WIDTH), (QUERY_HEADS * HEAD_SIZE) ** -0.5, 0.125, ((0, 4),))
    lengths = uneven_parts(key_list[6], NDOC, TOKENS, DOC_MAX, 2).astype(jnp.int32)
    return {"tokens": tokens, "norm_gain": norm_gain, "w_query": w_query, "key_weight": key_weight, "value_weight": value_weight, "w_out": w_out, "lengths": lengths}


epsilon = 1e-05
rope_base = 500000.0
masked = -1e+30

def doc_starts(lengths, positions):
    doc_ends = jnp.cumsum(lengths)
    closed = (doc_ends[None, :] <= positions[:, None]).astype(jnp.int32)
    return lax.optimization_barrier(jnp.sum(closed * lengths[None, :], axis=1)).astype(jnp.int32)

def rotate(vectors, offsets):
    half_width = vectors.shape[-1] // 2
    exponent = jnp.arange(half_width, dtype=jnp.float32) * (-2.0 / vectors.shape[-1])
    frequency = rope_base ** exponent
    angles = offsets.astype(jnp.float32)[:, None] * frequency[None, :]
    cos_part = jnp.cos(angles)[:, None, :]
    sin_part = jnp.sin(angles)[:, None, :]
    leading = vectors[..., :half_width]
    trailing = vectors[..., half_width:]
    return jnp.concatenate([leading * cos_part - trailing * sin_part, trailing * cos_part + leading * sin_part], axis=-1)

def project(tokens, norm_gain, w_query, key_weight, value_weight, positions, starts):
    count = tokens.shape[0]
    wide = tokens.astype(jnp.float32)
    inverse = lax.rsqrt(lax.optimization_barrier(jnp.mean(wide * wide, axis=1, keepdims=True)) + epsilon)
    normed = (wide * inverse * norm_gain[None, :]).astype(jnp.bfloat16)
    offsets = positions - starts
    query_rows = jnp.dot(normed, w_query, preferred_element_type=jnp.float32).reshape(count, -1, HEAD_SIZE)
    query_rows = rotate(query_rows, offsets).astype(jnp.bfloat16)
    key = jnp.dot(normed, key_weight, preferred_element_type=jnp.float32).reshape(count, -1, HEAD_SIZE)
    key = rotate(key, offsets).astype(jnp.bfloat16)
    value_rows = jnp.dot(normed, value_weight, preferred_element_type=jnp.float32).astype(jnp.bfloat16)
    return (query_rows, key.reshape(count, -1), value_rows)

def reference(tokens, norm_gain, w_query, key_weight, value_weight, w_out, lengths):
    total_count = tokens.shape[0]
    positions = jnp.arange(total_count, dtype=jnp.int32)
    starts = doc_starts(lengths, positions)
    query_rows, key, value_rows = project(tokens, norm_gain, w_query, key_weight, value_weight, positions, starts)
    block_index = min(512, total_count)
    window = min(DOC_MAX + block_index, total_count)
    group_count = QUERY_HEADS // KEY_VALUE_HEADS
    query_rows = query_rows.reshape(total_count // block_index, block_index, KEY_VALUE_HEADS, group_count, HEAD_SIZE)
    key = key.reshape(total_count, KEY_VALUE_HEADS, HEAD_SIZE)
    value_rows = value_rows.reshape(total_count, KEY_VALUE_HEADS, HEAD_SIZE)
    start_blocks = starts.reshape(total_count // block_index, block_index)
    scale = HEAD_SIZE ** (-0.5)

    def attend(pieces):
        index, query_block, start_block = pieces
        first = (index * block_index).astype(jnp.int32)
        key_first = jnp.clip(first + block_index - window, 0, total_count - window).astype(jnp.int32)
        key_block = lax.dynamic_slice_in_dim(key, key_first, window, 0)
        value_block = lax.dynamic_slice_in_dim(value_rows, key_first, window, 0)
        scores = jnp.einsum('qkgd,skd->qkgs', query_block.astype(jnp.float32), key_block.astype(jnp.float32)) * scale
        key_pos = key_first + jnp.arange(window, dtype=jnp.int32)
        query_pos = first + jnp.arange(block_index, dtype=jnp.int32)
        visible = (key_pos[None, :] >= start_block[:, None]) & (key_pos[None, :] <= query_pos[:, None])
        scores = jnp.where(visible[:, None, None, :], scores, masked)
        peak = lax.optimization_barrier(jnp.max(scores, axis=-1, keepdims=True))
        probs = jnp.exp(scores - peak)
        mass = lax.optimization_barrier(jnp.sum(probs, axis=-1, keepdims=True))
        weights = lax.optimization_barrier(probs.astype(jnp.bfloat16)).astype(jnp.float32)
        mixed = jnp.einsum('qkgs,skd->qkgd', weights, value_block.astype(jnp.float32)) / mass
        return mixed.reshape(block_index, QUERY_HEADS * HEAD_SIZE).astype(jnp.bfloat16)
    blocks = jnp.arange(total_count // block_index, dtype=jnp.int32)
    attended = lax.map(attend, (blocks, query_rows, start_blocks)).reshape(total_count, QUERY_HEADS * HEAD_SIZE)
    branch = jnp.dot(attended, w_out, preferred_element_type=jnp.float32)
    return (tokens.astype(jnp.float32) + branch).astype(jnp.bfloat16)
```

```python
import functools
import math

import jax
import jax.numpy as jnp
from jax import lax
from jax.experimental import pallas as pl
from jax.experimental.pallas import tpu as pltpu
from jax.sharding import PartitionSpec as P

HEAD_SIZE = 128
MESH = pl.DeviceIdType.MESH

epsilon = 1e-05
rope_base = 500000.0
masked = -1e30
initial_peak = -1e29


def doc_starts(lengths, positions):
    doc_ends = jnp.cumsum(lengths)
    closed = (doc_ends[None, :] <= positions[:, None]).astype(jnp.int32)
    return jnp.sum(closed * lengths[None, :], axis=1)


def flip(index, bits):
    low, high = index % 2, index // 2
    if bits & 1:
        low = 1 - low
    if bits & 2:
        high = 1 - high
    return high * 2 + low


def project_kernel(
    chunks, tokens, gain, cos_ref, sin_ref, wq, wk, wv,
    q_out, kv_out,
    held, normed, weight, raw, own_sem, weight_sem, send1, recv1, send2, recv2, send3, recv3,
):
    me = lax.axis_index("tensor")
    near, far = flip(me, 1), flip(me, 2)
    rows = tokens.shape[0]
    piece = rows // chunks
    heads = q_out.shape[0]
    q_width = wq.shape[1]
    kv_width = wk.shape[1]

    loads = [
        pltpu.make_async_copy(tokens, held.at[0], own_sem),
        pltpu.make_async_copy(wq, weight.at[:, pl.ds(0, q_width)], weight_sem.at[0]),
        pltpu.make_async_copy(wk, weight.at[:, pl.ds(q_width, kv_width)], weight_sem.at[1]),
        pltpu.make_async_copy(wv, weight.at[:, pl.ds(q_width + kv_width, kv_width)], weight_sem.at[2]),
    ]
    for load in loads:
        load.start()

    barrier = pltpu.get_barrier_semaphore()
    for other in (near, far):
        pl.semaphore_signal(barrier, inc=1, device_id={"tensor": other}, device_id_type=MESH)
    pl.semaphore_wait(barrier, 2)

    def remote(src, dst, send, recv, other):
        return pltpu.make_async_remote_copy(
            src_ref=src, dst_ref=dst, send_sem=send, recv_sem=recv,
            device_id={"tensor": other}, device_id_type=MESH,
        )

    cross = [
        remote(
            tokens.at[pl.ds(c * piece, piece), :], held.at[2, pl.ds(c * piece, piece), :],
            send2.at[c], recv2.at[c], far,
        )
        for c in range(chunks)
    ]
    for copy in cross:
        copy.start()
    sideways = remote(tokens, held.at[1], send1, recv1, near)
    sideways.start()

    def project(slot):
        block = flip(me, slot) if slot else me
        first = pl.multiple_of(block * rows, rows)
        wide = held[slot].astype(jnp.float32)
        inverse = lax.rsqrt(jnp.mean(wide * wide, axis=1, keepdims=True) + epsilon)
        normed[...] = (wide * inverse * gain[...]).astype(jnp.bfloat16)

        tile = 256
        @pl.loop(0, weight.shape[1] // tile)
        def _(n):
            columns = pl.ds(pl.multiple_of(n * tile, tile), tile)
            raw[:, columns] = jnp.dot(normed[...], weight[:, columns], preferred_element_type=jnp.float32)

        cos = cos_ref[pl.ds(first, rows), :]
        sin = sin_ref[pl.ds(first, rows), :]

        def rotated(index):
            part = raw[:, index * HEAD_SIZE:(index + 1) * HEAD_SIZE]
            return (part * cos + pltpu.roll(part, HEAD_SIZE // 2, 1) * sin).astype(jnp.bfloat16)

        for h in range(heads):
            q_out[h, pl.ds(first, rows), :] = rotated(h)
        kv_out[0, pl.ds(first, rows), :] = rotated(heads)
        kv_out[1, pl.ds(first, rows), :] = raw[:, (heads + 1) * HEAD_SIZE:].astype(jnp.bfloat16)

    for load in loads:
        load.wait()
    project(0)
    sideways.wait_recv()
    project(1)
    relays = []
    for c in range(chunks):
        cross[c].wait_recv()
        part = held.at[2, pl.ds(c * piece, piece), :]
        relay = remote(part, held.at[3, pl.ds(c * piece, piece), :], send3.at[c], recv3.at[c], near)
        relay.start()
        relays.append(relay)
    project(2)
    for relay in relays:
        relay.wait_recv()
    project(3)
    sideways.wait_send()
    for copy in cross + relays:
        copy.wait_send()


def project_call(tokens, gain, cos, sin, wq, wk, wv, tensor):
    rows, width = tokens.shape
    count = rows * tensor
    heads = wq.shape[1] // HEAD_SIZE
    total = wq.shape[1] + wk.shape[1] + wv.shape[1]
    chunks = 4
    any_spec = pl.BlockSpec(memory_space=pl.ANY)
    vmem = pl.BlockSpec(memory_space=pltpu.VMEM)
    return pl.pallas_call(
        functools.partial(project_kernel, chunks),
        out_shape=(
            jax.ShapeDtypeStruct((heads, count, HEAD_SIZE), jnp.bfloat16),
            jax.ShapeDtypeStruct((2, count, HEAD_SIZE), jnp.bfloat16),
        ),
        in_specs=[any_spec, vmem, vmem, vmem, any_spec, any_spec, any_spec],
        out_specs=(vmem, vmem),
        scratch_shapes=[
            pltpu.VMEM((4, rows, width), jnp.bfloat16),
            pltpu.VMEM((rows, width), jnp.bfloat16),
            pltpu.VMEM((width, total), jnp.bfloat16),
            pltpu.VMEM((rows, total), jnp.float32),
            pltpu.SemaphoreType.DMA,
            pltpu.SemaphoreType.DMA((3,)),
            pltpu.SemaphoreType.DMA,
            pltpu.SemaphoreType.DMA,
            pltpu.SemaphoreType.DMA((chunks,)),
            pltpu.SemaphoreType.DMA((chunks,)),
            pltpu.SemaphoreType.DMA((chunks,)),
            pltpu.SemaphoreType.DMA((chunks,)),
        ],
        compiler_params=pltpu.CompilerParams(
            collective_id=0, has_side_effects=True, vmem_limit_bytes=60 * 2**20
        ),
        name="gather_project",
    )(tokens, gain, cos, sin, wq, wk, wv)


def attend_kernel(
    dp, reach, chunks, q_ref, kv_ref, starts, tokens, w_out,
    out_ref,
    ring, peak, mass, summed, attended, weight, part_a, part_b, part_c, got_a, got_b, got_c, mine,
    load_sem, z_send, x_send, ring_recv, send_a, recv_a, send_b, recv_b, send_c, recv_c,
):
    me = lax.axis_index("tensor")
    here = lax.axis_index("dp")
    odd = here % 2
    heads, count, _ = q_ref.shape
    rows = count // 4
    near, far = flip(me, 1), flip(me, 2)
    partner = here + 1 - 2 * odd

    loads = [
        pltpu.make_async_copy(w_out, weight, load_sem.at[0]),
        pltpu.make_async_copy(tokens, mine, load_sem.at[1]),
    ]
    for load in loads:
        load.start()

    barrier = pltpu.get_barrier_semaphore()
    for other in (near, far):
        pl.semaphore_signal(barrier, inc=1, device_id={"tensor": other}, device_id_type=MESH)
    pl.semaphore_signal(barrier, inc=1, device_id={"dp": partner}, device_id_type=MESH)

    for other in ((here + 2) % dp, (here + dp - 2) % dp):
        pl.semaphore_signal(barrier, inc=1, device_id={"dp": other}, device_id_type=MESH)
    pl.semaphore_wait(barrier, 5)

    last_even = reach + 1 if reach % 2 else reach

    def along(src, j):
        return pltpu.make_async_remote_copy(
            src_ref=src, dst_ref=ring.at[j + 2], send_sem=z_send.at[j], recv_sem=ring_recv.at[j + 2],
            device_id={"dp": here + 2}, device_id_type=MESH,
        )

    def across(src, j):
        target = j + 1 - 2 * odd
        return pltpu.make_async_remote_copy(
            src_ref=src, dst_ref=ring.at[target], send_sem=x_send.at[j], recv_sem=ring_recv.at[target],
            device_id={"dp": partner}, device_id_type=MESH,
        )

    def goes_along(j):
        return (here + 2 < dp) & (j + 2 <= reach + odd) & (here >= j)

    def goes_across(j):
        target = j + 1 - 2 * odd
        return (target >= 1) & (target <= reach) & (here >= j)

    def forward(src, j):
        @pl.when(goes_along(j))
        def _():
            along(src, j).start()

        @pl.when(goes_across(j))
        def _():
            across(src, j).start()

    def settle(j):
        @pl.when(goes_along(j))
        def _():
            along(kv_ref, j).wait_send()

        @pl.when(goes_across(j))
        def _():
            across(kv_ref, j).wait_send()

    def arrive(j):
        pltpu.make_async_remote_copy(
            src_ref=kv_ref, dst_ref=ring.at[j], send_sem=z_send.at[j], recv_sem=ring_recv.at[j],
            device_id={"dp": partner}, device_id_type=MESH,
        ).wait_recv()

    forward(kv_ref, 0)

    scale = HEAD_SIZE ** (-0.5) * math.log2(math.e)
    block = 256
    tiles = heads * count // block
    per_head = count // block

    def scores_of(h, row, keys):
        scores = lax.dot_general(
            q_ref[h, pl.ds(row, block), :], keys, (((1,), (1,)), ((), ())),
            preferred_element_type=jnp.float32,
        )
        return scores * scale

    @pl.loop(0, tiles)
    def _(i):
        h, row = i // per_head, pl.multiple_of(i % per_head * block, block)
        scores = scores_of(h, row, kv_ref[0])
        key_pos = lax.broadcasted_iota(jnp.int32, (block, count), 1)
        query_pos = row + lax.broadcasted_iota(jnp.int32, (block, 1), 0)
        begin = starts[pl.ds(row, block), :] - here * count
        scores = jnp.where((key_pos >= begin) & (key_pos <= query_pos), scores, masked)
        top = jnp.max(scores, axis=1, keepdims=True)
        probs = jnp.exp2(scores - top)
        peak[h, pl.ds(row, block), :] = top
        mass[h, pl.ds(row, block), :] = jnp.sum(probs, axis=1, keepdims=True)
        summed[h, pl.ds(row, block), :] = jnp.dot(
            probs.astype(jnp.bfloat16), kv_ref[1], preferred_element_type=jnp.float32
        )

    def fold(j):
        @pl.loop(0, tiles)
        def _(i):
            h, row = i // per_head, pl.multiple_of(i % per_head * block, block)
            scores = scores_of(h, row, ring[j, 0])
            key_pos = lax.broadcasted_iota(jnp.int32, (block, count), 1)
            begin = starts[pl.ds(row, block), :] - (here - j) * count
            scores = jnp.where(key_pos >= begin, scores, masked)
            old = peak[h, pl.ds(row, block), :]
            top = jnp.maximum(old, jnp.max(scores, axis=1, keepdims=True))
            shrink = jnp.exp2(old - top)
            probs = jnp.exp2(scores - top)
            peak[h, pl.ds(row, block), :] = top
            mass[h, pl.ds(row, block), :] = mass[h, pl.ds(row, block), :] * shrink + jnp.sum(
                probs, axis=1, keepdims=True
            )
            summed[h, pl.ds(row, block), :] = summed[h, pl.ds(row, block), :] * shrink + jnp.dot(
                probs.astype(jnp.bfloat16), ring[j, 1], preferred_element_type=jnp.float32
            )

    @pl.loop(0, last_even // 2)
    def _(step):
        even = 2 * step + 2

        @pl.when((here >= even) & (even <= reach + odd))
        def _():
            arrive(even)
            forward(ring.at[even], even)

        @pl.when((here >= even) & (even <= reach))
        def _():
            fold(even)

        @pl.when(here >= even - 1)
        def _():
            arrive(even - 1)
            fold(even - 1)

    for h in range(heads):
        attended[:, h * HEAD_SIZE:(h + 1) * HEAD_SIZE] = (summed[h] / mass[h]).astype(jnp.bfloat16)

    @pl.loop(0, last_even // 2 + 1)
    def _(step):
        @pl.when(2 * step <= reach + odd)
        def _():
            settle(2 * step)

    for load in loads:
        load.wait()
    wide = weight.shape[1] // chunks

    def share(block_of, c):
        first = pl.multiple_of(block_of * rows, rows)
        columns = pl.ds(pl.multiple_of(c * wide, wide), wide)
        return jnp.dot(attended[pl.ds(first, rows), :], weight[:, columns], preferred_element_type=jnp.float32)

    def hand(src, dst, send, recv, c, other):
        return pltpu.make_async_remote_copy(
            src_ref=src.at[c], dst_ref=dst.at[c], send_sem=send.at[c], recv_sem=recv.at[c],
            device_id={"tensor": other}, device_id_type=MESH,
        )

    copy_a = lambda c: hand(part_a, got_a, send_a, recv_a, c, near)
    copy_b = lambda c: hand(part_b, got_b, send_b, recv_b, c, far)
    copy_c = lambda c: hand(part_c, got_c, send_c, recv_c, c, near)

    @pl.loop(0, chunks)
    def _(c):
        part_a[c] = share(flip(me, 3), c).astype(jnp.bfloat16)
        copy_a(c).start()

    @pl.loop(0, chunks)
    def _(c):
        own = share(far, c)
        copy_a(c).wait_recv()
        part_b[c] = (own + got_a[c].astype(jnp.float32)).astype(jnp.bfloat16)
        copy_b(c).start()

    @pl.loop(0, chunks)
    def _(c):
        part_c[c] = share(near, c).astype(jnp.bfloat16)
        copy_c(c).start()

    @pl.loop(0, chunks)
    def _(c):
        columns = pl.ds(pl.multiple_of(c * wide, wide), wide)
        total = share(me, c) + mine[:, columns].astype(jnp.float32)
        copy_c(c).wait_recv()
        total = total + got_c[c].astype(jnp.float32)
        copy_b(c).wait_recv()
        out_ref[:, columns] = (total + got_b[c].astype(jnp.float32)).astype(jnp.bfloat16)

    @pl.loop(0, chunks)
    def _(c):
        copy_a(c).wait_send()
        copy_b(c).wait_send()
        copy_c(c).wait_send()


def attend_call(q, kv, starts, tokens, w_out, dp):
    heads, count, _ = q.shape
    rows, width = tokens.shape
    reach = min(dp // 2 + 1, dp - 1)
    slots = reach + 2
    chunks = 8
    any_spec = pl.BlockSpec(memory_space=pl.ANY)
    vmem = pl.BlockSpec(memory_space=pltpu.VMEM)
    pieces = pltpu.VMEM((chunks, rows, width // chunks), jnp.bfloat16)
    sems = pltpu.SemaphoreType.DMA((chunks,))
    return pl.pallas_call(
        functools.partial(attend_kernel, dp, reach, chunks),
        out_shape=jax.ShapeDtypeStruct((rows, width), jnp.bfloat16),
        in_specs=[vmem, vmem, vmem, any_spec, any_spec],
        out_specs=vmem,
        scratch_shapes=[
            pltpu.VMEM((slots, 2, count, HEAD_SIZE), jnp.bfloat16),
            pltpu.VMEM((heads, count, 1), jnp.float32),
            pltpu.VMEM((heads, count, 1), jnp.float32),
            pltpu.VMEM((heads, count, HEAD_SIZE), jnp.float32),
            pltpu.VMEM((count, heads * HEAD_SIZE), jnp.bfloat16),
            pltpu.VMEM(w_out.shape, jnp.bfloat16),
            pieces, pieces, pieces, pieces, pieces, pieces,
            pltpu.VMEM((rows, width), jnp.bfloat16),
            pltpu.SemaphoreType.DMA((2,)),
            pltpu.SemaphoreType.DMA((slots,)),
            pltpu.SemaphoreType.DMA((slots,)),
            pltpu.SemaphoreType.DMA((slots,)),
            sems, sems, sems, sems, sems, sems,
        ],
        compiler_params=pltpu.CompilerParams(
            collective_id=1, has_side_effects=True, vmem_limit_bytes=60 * 2**20
        ),
        name="attend_scatter",
    )(q, kv, starts, tokens, w_out)


def body(tokens, norm_gain, w_query, key_weight, value_weight, w_out, lengths):
    tensor = lax.axis_size("tensor")
    dp = lax.axis_size("dp")
    count = tokens.shape[0] * tensor
    positions = lax.axis_index("dp") * count + jnp.arange(count, dtype=jnp.int32)
    starts = doc_starts(lengths, positions)
    half = HEAD_SIZE // 2
    exponent = jnp.arange(half, dtype=jnp.float32) * (-2.0 / HEAD_SIZE)
    angles = (positions - starts).astype(jnp.float32)[:, None] * (rope_base**exponent)[None, :]
    cos, sin = jnp.cos(angles), jnp.sin(angles)
    cos = jnp.concatenate([cos, cos], axis=1)
    sin = jnp.concatenate([-sin, sin], axis=1)
    q, kv = project_call(
        tokens, norm_gain[None, :], cos, sin, w_query, key_weight, value_weight, tensor
    )
    return attend_call(q, kv, starts[:, None], tokens, w_out, dp)


def solution(mesh):
    in_specs = (
        P(("dp", "tensor"), None),
        P(),
        P(None, "tensor"),
        P(None, "tensor"),
        P(None, "tensor"),
        P("tensor", None),
        P(),
    )
    out_specs = P(("dp", "tensor"), None)
    return jax.shard_map(body, mesh=mesh, in_specs=in_specs, out_specs=out_specs, check_vma=False)
```

```python
import functools
import math

import jax
import jax.numpy as jnp
from jax import lax
from jax.experimental import pallas as pl
from jax.experimental.pallas import tpu as pltpu
from jax.sharding import PartitionSpec as P

HEAD_SIZE = 128
MESH = pl.DeviceIdType.MESH

epsilon = 1e-05
rope_base = 500000.0
masked = -1e30


def flip(index, bits):
    low, high = index % 2, index // 2
    if bits & 1:
        low = 1 - low
    if bits & 2:
        high = 1 - high
    return high * 2 + low


def kernel(
    dp, reach, pieces, chunks,
    lengths, gain, frequency, tokens, wq, wk, wv, w_out,
    out_ref,
    held, normed, weight, raw, cos_ref, sin_ref, query, keys, peak, mass, summed, attended, weight_out,
    part_a, part_b, part_c, got_a, got_b, got_c,
    load_sem, send1, recv1, send2, recv2, send3, recv3, z_send, x_send, ring_recv,
    send_a, recv_a, send_b, recv_b, send_c, recv_c,
):
    me = lax.axis_index("tensor")
    here = lax.axis_index("dp")
    odd = here % 2
    partner = here + 1 - 2 * odd
    near, far = flip(me, 1), flip(me, 2)
    rows = tokens.shape[0]
    count = 4 * rows
    half = 2 * rows
    heads = query.shape[0]
    lanes = HEAD_SIZE
    q_width, kv_width = wq.shape[1], wk.shape[1]
    last_even = reach + 1 if reach % 2 else reach

    loads = [
        pltpu.make_async_copy(tokens, held.at[0], load_sem.at[0]),
        pltpu.make_async_copy(wq, weight.at[:, pl.ds(0, q_width)], load_sem.at[1]),
        pltpu.make_async_copy(wk, weight.at[:, pl.ds(q_width, kv_width)], load_sem.at[2]),
        pltpu.make_async_copy(wv, weight.at[:, pl.ds(q_width + kv_width, kv_width)], load_sem.at[3]),
    ]
    load_out = pltpu.make_async_copy(w_out, weight_out, load_sem.at[4])

    barrier = pltpu.get_barrier_semaphore()
    for other in (near, far):
        pl.semaphore_signal(barrier, inc=1, device_id={"tensor": other}, device_id_type=MESH)
    for other in (partner, (here + 2) % dp, (here + dp - 2) % dp):
        pl.semaphore_signal(barrier, inc=1, device_id={"dp": other}, device_id_type=MESH)
    for load in loads:
        load.start()
    pl.semaphore_wait(barrier, 5)

    def remote(src, dst, send, recv, axis, other):
        return pltpu.make_async_remote_copy(
            src_ref=src, dst_ref=dst, send_sem=send, recv_sem=recv,
            device_id={axis: other}, device_id_type=MESH,
        )

    piece = rows // pieces
    cross, relays = [], []
    for c in range(pieces):
        span = pl.ds(c * piece, piece)
        cross.append(remote(tokens.at[span, :], held.at[2, span, :], send2.at[c], recv2.at[c], "tensor", far))
        relays.append(remote(held.at[2, span, :], held.at[3, span, :], send3.at[c], recv3.at[c], "tensor", near))
    for copy in cross:
        copy.start()
    sideways = remote(tokens, held.at[1], send1, recv1, "tensor", near)
    sideways.start()
    load_out.start()

    lane = lax.broadcasted_iota(jnp.int32, (1, lanes), 1)
    begin = jnp.zeros((1, lanes), jnp.int32)
    end = jnp.zeros((1, lanes), jnp.int32)
    total = jnp.int32(0)
    for e in range(lengths.shape[0]):
        begin = jnp.where(lane == e, total, begin)
        total = total + lengths[e]
        end = jnp.where(lane == e, total, end)
    sign = jnp.where(lane < lanes // 2, -1.0, 1.0)

    def inside(first, number):
        position = first + lax.broadcasted_iota(jnp.int32, (number, 1), 0)
        return position, (position >= begin) & (position < end)

    @pl.loop(0, 4)
    def _(b):
        first = pl.multiple_of(b * rows, rows)
        position, belongs = inside(here * count + first, rows)
        start = jnp.sum(jnp.where(belongs, begin.astype(jnp.float32), 0.0), axis=1, keepdims=True)
        angle = (position.astype(jnp.float32) - start) * frequency[...]
        cos_ref[pl.ds(first, rows), :] = jnp.cos(angle)
        sin_ref[pl.ds(first, rows), :] = jnp.sin(angle) * sign
        mark = jnp.where(belongs, 1.0, 0.0).astype(jnp.bfloat16)
        for h in range(heads):
            query[h, pl.ds(first, rows), 0:lanes] = mark

    for h in range(2):
        pair = me // 2 if h == 0 else 1 - me // 2

        @pl.loop(0, reach + 1)
        def _(j):
            slot = pl.ds(pl.multiple_of(j * half, half), half)
            _, belongs = inside((here - j) * count + pair * half, half)
            keys[h, slot, 0:lanes] = jnp.where(belongs, 0.0, masked).astype(jnp.bfloat16)

            @pl.when(here < j)
            def _():
                keys[h, slot, lanes:3 * lanes] = jnp.zeros((half, 2 * lanes), jnp.bfloat16)

    def part(j, h):
        return keys.at[h, pl.ds(pl.multiple_of(j * half, half), half), pl.ds(lanes, 2 * lanes)]

    def along(j, h):
        return remote(part(j, h), part(j + 2, h), z_send.at[j, h], ring_recv.at[j + 2, h], "dp", here + 2)

    def across(j, h):
        target = j + 1 - 2 * odd
        return remote(part(j, h), part(target, h), x_send.at[j, h], ring_recv.at[target, h], "dp", partner)

    def goes_along(j):
        return (here + 2 < dp) & (j + 2 <= reach + odd) & (here >= j)

    def goes_across(j):
        target = j + 1 - 2 * odd
        return (target >= 1) & (target <= reach) & (here >= j)

    def forward(j, h):
        @pl.when(goes_along(j))
        def _():
            along(j, h).start()

        @pl.when(goes_across(j))
        def _():
            across(j, h).start()

    def settle(j, h):
        @pl.when(goes_along(j))
        def _():
            along(j, h).wait_send()

        @pl.when(goes_across(j))
        def _():
            across(j, h).wait_send()

    def arrive(j, h):
        remote(part(j, h), part(j, h), z_send.at[j, h], ring_recv.at[j, h], "dp", partner).wait_recv()

    def pass_on(j, h):
        @pl.when((here >= j) & (j <= reach + odd))
        def _():
            arrive(j, h)
            forward(j, h)

    def odd_arrivals(h):
        for j in range(1, reach + 1, 2):
            @pl.when(here >= j)
            def _():
                arrive(j, h)

    def project(slot):
        block = flip(me, slot)
        first = pl.multiple_of(block * rows, rows)
        wide = held[slot].astype(jnp.float32)
        inverse = lax.rsqrt(jnp.mean(wide * wide, axis=1, keepdims=True) + epsilon)
        normed[...] = (wide * inverse * gain[...]).astype(jnp.bfloat16)
        tile = 256

        @pl.loop(0, weight.shape[1] // tile)
        def _(n):
            columns = pl.ds(pl.multiple_of(n * tile, tile), tile)
            raw[:, columns] = jnp.dot(normed[...], weight[:, columns], preferred_element_type=jnp.float32)

        cos = cos_ref[pl.ds(first, rows), :]
        sin = sin_ref[pl.ds(first, rows), :]

        def rotated(index):
            entry = raw[:, index * lanes:(index + 1) * lanes]
            return (entry * cos + pltpu.roll(entry, lanes // 2, 1) * sin).astype(jnp.bfloat16)

        for h in range(heads):
            query[h, pl.ds(first, rows), lanes:2 * lanes] = rotated(h)
        place = pl.ds(pl.multiple_of(block % 2 * rows, rows), rows)
        keys[slot // 2, place, lanes:2 * lanes] = rotated(heads)
        keys[slot // 2, place, 2 * lanes:3 * lanes] = raw[:, (heads + 1) * lanes:].astype(jnp.bfloat16)

    scale = HEAD_SIZE ** (-0.5) * math.log2(math.e)
    seen = (reach + 1) * half

    def fold(slot, h, opening):
        first = pl.multiple_of(flip(me, slot) * rows, rows)
        span = pl.ds(first, rows)
        pair = me // 2 if h == 0 else 1 - me // 2
        key_pos = pair * half + lax.broadcasted_iota(jnp.int32, (rows, half), 1)
        query_pos = first + lax.broadcasted_iota(jnp.int32, (rows, 1), 0)
        causal = key_pos <= query_pos

        def one(g):
            scores = lax.dot_general(
                query[g, span, :], keys[h, 0:seen, 0:2 * lanes], (((1,), (1,)), ((), ())),
                preferred_element_type=jnp.float32,
            )
            scores = jnp.concatenate(
                [jnp.where(causal, scores[:, :half], masked), scores[:, half:]], axis=1
            )
            top = jnp.max(scores, axis=1, keepdims=True)
            if not opening:
                old = peak[g, span, :]
                top = jnp.maximum(old, top)
            else:
                top = jnp.maximum(top, -1e29)
            probs = jnp.exp2(scores * scale - top * scale)
            added = jnp.sum(probs, axis=1, keepdims=True)
            update = jnp.dot(
                probs.astype(jnp.bfloat16), keys[h, 0:seen, 2 * lanes:3 * lanes],
                preferred_element_type=jnp.float32,
            )
            if opening:
                peak[g, span, :] = top
                mass[g, span, :] = added
                summed[g, span, :] = update
            else:
                shrink = jnp.exp2((old - top) * scale)
                whole = mass[g, span, :] * shrink + added
                result = (summed[g, span, :] * shrink + update) / whole
                attended[g, span, :] = result.astype(jnp.bfloat16)

        @pl.loop(0, heads // 2)
        def _(i):
            one(2 * i)
            one(2 * i + 1)

    for load in loads:
        load.wait()
    project(0)
    sideways.wait_recv()
    project(1)
    forward(0, 0)
    hops = list(range(2, last_even + 1, 2))
    for c in range(pieces):
        cross[c].wait_recv()
        relays[c].start()
        share_of = hops[len(hops) * c // pieces:len(hops) * (c + 1) // pieces]
        for j in share_of:
            pass_on(j, 0)
    project(2)
    for relay in relays:
        relay.wait_recv()
    project(3)
    forward(0, 1)

    odd_arrivals(0)
    order = (0, 1, 2, 3)
    for n in range(4):
        fold(order[n], 0, True)
        for j in hops[len(hops) * n // 4:len(hops) * (n + 1) // 4]:
            pass_on(j, 1)
    odd_arrivals(1)

    load_out.wait()
    wide = weight_out.shape[1] // chunks

    def share(block_of, c):
        first = pl.multiple_of(block_of * rows, rows)
        columns = pl.ds(pl.multiple_of(c * wide, wide), wide)
        joined = jnp.concatenate([attended[g, pl.ds(first, rows), :] for g in range(heads)], axis=1)
        return jnp.dot(joined, weight_out[:, columns], preferred_element_type=jnp.float32)

    def hand(src, dst, send, recv, c, other):
        return remote(src.at[c], dst.at[c], send.at[c], recv.at[c], "tensor", other)

    copy_a = lambda c: hand(part_a, got_a, send_a, recv_a, c, near)
    copy_b = lambda c: hand(part_b, got_b, send_b, recv_b, c, far)
    copy_c = lambda c: hand(part_c, got_c, send_c, recv_c, c, near)

    fold(3, 1, False)

    @pl.loop(0, chunks)
    def _(c):
        part_a[c] = share(flip(me, 3), c).astype(jnp.bfloat16)
        copy_a(c).start()

    fold(2, 1, False)

    @pl.loop(0, chunks)
    def _(c):
        own = share(far, c)
        copy_a(c).wait_recv()
        part_b[c] = (own + got_a[c].astype(jnp.float32)).astype(jnp.bfloat16)
        copy_b(c).start()

    fold(1, 1, False)

    @pl.loop(0, chunks)
    def _(c):
        part_c[c] = share(near, c).astype(jnp.bfloat16)
        copy_c(c).start()

    fold(0, 1, False)

    @pl.loop(0, chunks)
    def _(c):
        columns = pl.ds(pl.multiple_of(c * wide, wide), wide)
        result = share(me, c) + held[0, :, columns].astype(jnp.float32)
        copy_c(c).wait_recv()
        result = result + got_c[c].astype(jnp.float32)
        copy_b(c).wait_recv()
        out_ref[:, columns] = (result + got_b[c].astype(jnp.float32)).astype(jnp.bfloat16)

    @pl.loop(0, chunks)
    def _(c):
        copy_a(c).wait_send()
        copy_b(c).wait_send()
        copy_c(c).wait_send()

    sideways.wait_send()
    for copy in cross + relays:
        copy.wait_send()
    for h in range(2):
        for j in range(0, last_even + 1, 2):
            @pl.when(j <= reach + odd)
            def _():
                settle(j, h)


def body(tokens, norm_gain, w_query, key_weight, value_weight, w_out, lengths):
    dp = lax.axis_size("dp")
    rows, width = tokens.shape
    count = 4 * rows
    heads = w_query.shape[1] // HEAD_SIZE
    total = w_query.shape[1] + key_weight.shape[1] + value_weight.shape[1]
    reach = min(dp // 2 + 1, dp - 1)
    slots = reach + 2
    pieces, chunks = 4, 8
    exponent = jnp.arange(HEAD_SIZE // 2, dtype=jnp.float32) * (-2.0 / HEAD_SIZE)
    frequency = jnp.tile(rope_base**exponent, 2)[None, :]
    any_spec = pl.BlockSpec(memory_space=pl.ANY)
    vmem = pl.BlockSpec(memory_space=pltpu.VMEM)
    smem = pl.BlockSpec(memory_space=pltpu.SMEM)
    bf16, f32 = jnp.bfloat16, jnp.float32
    part = pltpu.VMEM((chunks, rows, width // chunks), bf16)
    dma = pltpu.SemaphoreType.DMA
    return pl.pallas_call(
        functools.partial(kernel, dp, reach, pieces, chunks),
        out_shape=jax.ShapeDtypeStruct((rows, width), bf16),
        in_specs=[smem, vmem, vmem, any_spec, any_spec, any_spec, any_spec, any_spec],
        out_specs=vmem,
        scratch_shapes=[
            pltpu.VMEM((4, rows, width), bf16),
            pltpu.VMEM((rows, width), bf16),
            pltpu.VMEM((width, total), bf16),
            pltpu.VMEM((rows, total), f32),
            pltpu.VMEM((count, HEAD_SIZE), f32),
            pltpu.VMEM((count, HEAD_SIZE), f32),
            pltpu.VMEM((heads, count, 2 * HEAD_SIZE), bf16),
            pltpu.VMEM((2, slots * 2 * rows, 3 * HEAD_SIZE), bf16),
            pltpu.VMEM((heads, count, 1), f32),
            pltpu.VMEM((heads, count, 1), f32),
            pltpu.VMEM((heads, count, HEAD_SIZE), f32),
            pltpu.VMEM((heads, count, HEAD_SIZE), bf16),
            pltpu.VMEM(w_out.shape, bf16),
            part, part, part, part, part, part,
            dma((5,)), dma, dma,
            dma((pieces,)), dma((pieces,)), dma((pieces,)), dma((pieces,)),
            dma((slots, 2)), dma((slots, 2)), dma((slots, 2)),
            dma((chunks,)), dma((chunks,)), dma((chunks,)), dma((chunks,)), dma((chunks,)), dma((chunks,)),
        ],
        compiler_params=pltpu.CompilerParams(
            collective_id=0, has_side_effects=True, vmem_limit_bytes=62 * 2**20
        ),
        name="attention_block",
    )(lengths, norm_gain[None, :], frequency, tokens, w_query, key_weight, value_weight, w_out)


def solution(mesh):
    in_specs = (
        P(("dp", "tensor"), None),
        P(),
        P(None, "tensor"),
        P(None, "tensor"),
        P(None, "tensor"),
        P("tensor", None),
        P(),
    )
    out_specs = P(("dp", "tensor"), None)
    return jax.shard_map(body, mesh=mesh, in_specs=in_specs, out_specs=out_specs, check_vma=False)
```

```python
import functools
import math

import jax
import jax.numpy as jnp
from jax import lax
from jax.experimental import pallas as pl
from jax.experimental.pallas import tpu as pltpu
from jax.sharding import PartitionSpec as P

HEAD_SIZE = 128
MESH = pl.DeviceIdType.MESH

epsilon = 1e-05
rope_base = 500000.0
masked = -1e30


def flip(index, bits):
    low, high = index % 2, index // 2
    if bits & 1:
        low = 1 - low
    if bits & 2:
        high = 1 - high
    return high * 2 + low


def kernel(
    dp, reach, pieces, chunks,
    lengths, gain, frequency, tokens, wq, wk, wv, w_out,
    out_ref,
    held, normed, weight, raw, cos_ref, sin_ref, query, keys_near, keys_first, keys_last, peak, mass, summed, attended, weight_out,
    part_a, part_b, part_c, got_a, got_b, got_c,
    load_sem, send1, recv1, send2, recv2, send3, recv3, z_send, x_send, d_send, ring_recv,
    send_a, recv_a, send_b, recv_b, send_c, recv_c,
):
    me = lax.axis_index("tensor")
    here = lax.axis_index("dp")
    odd = here % 2
    partner = here + 1 - 2 * odd
    near, far = flip(me, 1), flip(me, 2)
    rows = tokens.shape[0]
    count = 4 * rows
    heads = query.shape[0]
    lanes = HEAD_SIZE
    q_width, kv_width = wq.shape[1], wk.shape[1]
    last_even = reach - reach % 2
    groups = (keys_near, keys_first, keys_last)
    sizes = (2 * rows, rows, rows)
    batch = rows // 2

    loads = [
        pltpu.make_async_copy(tokens, held.at[0], load_sem.at[0]),
        pltpu.make_async_copy(wq, weight.at[:, pl.ds(0, q_width)], load_sem.at[1]),
        pltpu.make_async_copy(wk, weight.at[:, pl.ds(q_width, kv_width)], load_sem.at[2]),
        pltpu.make_async_copy(wv, weight.at[:, pl.ds(q_width + kv_width, kv_width)], load_sem.at[3]),
    ]
    load_out = pltpu.make_async_copy(w_out, weight_out, load_sem.at[4])

    barrier = pltpu.get_barrier_semaphore()
    for other in (near, far):
        pl.semaphore_signal(barrier, inc=1, device_id={"tensor": other}, device_id_type=MESH)
    ways = (partner, (here + 2) % dp, (here + dp - 2) % dp, (here + reach) % dp, (here + dp - reach) % dp)
    for other in ways:
        pl.semaphore_signal(barrier, inc=1, device_id={"dp": other}, device_id_type=MESH)
    for load in loads:
        load.start()
    pl.semaphore_wait(barrier, 7)

    def remote(src, dst, send, recv, axis, other):
        return pltpu.make_async_remote_copy(
            src_ref=src, dst_ref=dst, send_sem=send, recv_sem=recv,
            device_id={axis: other}, device_id_type=MESH,
        )

    piece = rows // pieces
    cross, relays = [], []
    for c in range(pieces):
        span = pl.ds(c * piece, piece)
        cross.append(remote(tokens.at[span, :], held.at[2, span, :], send2.at[c], recv2.at[c], "tensor", far))
        relays.append(remote(held.at[2, span, :], held.at[3, span, :], send3.at[c], recv3.at[c], "tensor", near))
    for copy in cross:
        copy.start()
    sideways = remote(tokens, held.at[1], send1, recv1, "tensor", near)
    sideways.start()
    load_out.start()

    lane = lax.broadcasted_iota(jnp.int32, (1, lanes), 1)
    begin = jnp.zeros((1, lanes), jnp.int32)
    end = jnp.zeros((1, lanes), jnp.int32)
    total = jnp.int32(0)
    for e in range(lengths.shape[0]):
        begin = jnp.where(lane == e, total, begin)
        total = total + lengths[e]
        end = jnp.where(lane == e, total, end)
    sign = jnp.where(lane < lanes // 2, -1.0, 1.0)

    def inside(position):
        return position, (position >= begin) & (position < end)

    @pl.loop(0, 4)
    def _(b):
        first = pl.multiple_of(b * rows, rows)
        position, belongs = inside(here * count + first + lax.broadcasted_iota(jnp.int32, (rows, 1), 0))
        start = jnp.sum(jnp.where(belongs, begin.astype(jnp.float32), 0.0), axis=1, keepdims=True)
        angle = (position.astype(jnp.float32) - start) * frequency[...]
        cos_ref[pl.ds(first, rows), :] = jnp.cos(angle)
        sin_ref[pl.ds(first, rows), :] = jnp.sin(angle) * sign
        mark = jnp.where(belongs, 1.0, 0.0).astype(jnp.bfloat16)
        for h in range(heads):
            query[h, pl.ds(first, rows), 0:lanes] = mark

    def places(h, index):
        if h == 0:
            return me // 2 * (2 * rows) + index
        skip = (h - 1) * batch
        return index + skip + jnp.where(index < batch, far * rows, flip(me, 3) * rows - batch)

    for h in range(3):
        size = sizes[h]

        @pl.loop(0, reach + 1)
        def _(j):
            slot = pl.ds(pl.multiple_of(j * size, size), size)
            place = places(h, lax.broadcasted_iota(jnp.int32, (size, 1), 0))
            _, belongs = inside((here - j) * count + place)
            groups[h][slot, 0:lanes] = jnp.where(belongs, 0.0, masked).astype(jnp.bfloat16)

            @pl.when(here < j)
            def _():
                groups[h][slot, lanes:3 * lanes] = jnp.zeros((size, 2 * lanes), jnp.bfloat16)

    def part(j, h):
        size = sizes[h]
        return groups[h].at[pl.ds(pl.multiple_of(j * size, size), size), pl.ds(lanes, 2 * lanes)]

    def along(j, h):
        return remote(part(j, h), part(j + 2, h), z_send.at[j, h], ring_recv.at[j + 2, h], "dp", here + 2)

    def across(j, h):
        target = j + 1 - 2 * odd
        return remote(part(j, h), part(target, h), x_send.at[j, h], ring_recv.at[target, h], "dp", partner)

    direct_used = reach % 2 == 1
    goes_direct = (odd == 1) & (here + reach < dp)

    def direct(h):
        return remote(part(0, h), part(reach, h), d_send.at[h], ring_recv.at[reach, h], "dp", here + reach)

    def goes_along(j):
        return (here + 2 < dp) & (here >= j)

    def goes_across(j):
        target = j + 1 - 2 * odd
        return (target >= 1) & (target <= reach) & (here >= j)

    def forward(j, h):
        if j == 0 and direct_used:
            @pl.when(goes_direct)
            def _():
                direct(h).start()

        if j + 2 <= reach:
            @pl.when(goes_along(j))
            def _():
                along(j, h).start()

        @pl.when(goes_across(j))
        def _():
            across(j, h).start()

    def settle(j, h):
        if j == 0 and direct_used:
            @pl.when(goes_direct)
            def _():
                direct(h).wait_send()

        if j + 2 <= reach:
            @pl.when(goes_along(j))
            def _():
                along(j, h).wait_send()

        @pl.when(goes_across(j))
        def _():
            across(j, h).wait_send()

    def arrive(j, h):
        remote(part(j, h), part(j, h), z_send.at[j, h], ring_recv.at[j, h], "dp", partner).wait_recv()

    def pass_on(j, h):
        @pl.when(here >= j)
        def _():
            arrive(j, h)
            forward(j, h)

    def odd_arrivals(h):
        for j in range(1, reach + 1, 2):
            @pl.when(here >= j)
            def _():
                arrive(j, h)

    def project(h, parts):
        row = 0
        for slot, skip, number in parts:
            rows_of = held[slot, skip:skip + number, :].astype(jnp.float32)
            inverse = lax.rsqrt(jnp.mean(rows_of * rows_of, axis=1, keepdims=True) + epsilon)
            normed[row:row + number, :] = (rows_of * inverse * gain[...]).astype(jnp.bfloat16)
            row += number
        tile = 256

        @pl.loop(0, weight.shape[1] // tile)
        def _(n):
            columns = pl.ds(pl.multiple_of(n * tile, tile), tile)
            raw[:, columns] = jnp.dot(normed[...], weight[:, columns], preferred_element_type=jnp.float32)

        row = 0
        for slot, skip, number in parts:
            block = flip(me, slot)
            here_rows = pl.ds(pl.multiple_of(block * rows + skip, number), number)
            cos, sin = cos_ref[here_rows, :], sin_ref[here_rows, :]

            def rotated(index):
                entry = raw[row:row + number, index * lanes:(index + 1) * lanes]
                return (entry * cos + pltpu.roll(entry, lanes // 2, 1) * sin).astype(jnp.bfloat16)

            for g in range(heads):
                query[g, here_rows, lanes:2 * lanes] = rotated(g)
            place = pl.ds(pl.multiple_of(block % 2 * rows, rows), rows) if h == 0 else pl.ds(row, number)
            groups[h][place, lanes:2 * lanes] = rotated(heads)
            groups[h][place, 2 * lanes:3 * lanes] = raw[row:row + number, (heads + 1) * lanes:].astype(jnp.bfloat16)
            row += number

    scale = HEAD_SIZE ** (-0.5) * math.log2(math.e)

    def fold(slot, h, opening=False, closing=False):
        size = sizes[h]
        store = groups[h]
        first = pl.multiple_of(flip(me, slot) * rows, rows)
        span = pl.ds(first, rows)
        key_pos = places(h, lax.broadcasted_iota(jnp.int32, (rows, size), 1))
        query_pos = first + lax.broadcasted_iota(jnp.int32, (rows, 1), 0)
        causal = key_pos <= query_pos

        def one(g):
            scores = lax.dot_general(
                query[g, span, :], store[:, 0:2 * lanes], (((1,), (1,)), ((), ())),
                preferred_element_type=jnp.float32,
            )
            scores = jnp.concatenate(
                [jnp.where(causal, scores[:, :size], masked), scores[:, size:]], axis=1
            )
            top = jnp.max(scores, axis=1, keepdims=True)
            if not opening:
                old = peak[g, span, :]
                top = jnp.maximum(old, top)
            else:
                top = jnp.maximum(top, -1e29)
            probs = jnp.exp2(scores * scale - top * scale)
            added = jnp.sum(probs, axis=1, keepdims=True)
            update = jnp.dot(
                probs.astype(jnp.bfloat16), store[:, 2 * lanes:3 * lanes],
                preferred_element_type=jnp.float32,
            )
            if opening:
                peak[g, span, :] = top
                mass[g, span, :] = added
                summed[g, span, :] = update
            else:
                shrink = jnp.exp2((old - top) * scale)
                whole = mass[g, span, :] * shrink + added
                result = summed[g, span, :] * shrink + update
                if closing:
                    attended[g, span, :] = (result / whole).astype(jnp.bfloat16)
                else:
                    peak[g, span, :] = top
                    mass[g, span, :] = whole
                    summed[g, span, :] = result

        @pl.loop(0, heads // 2)
        def _(i):
            one(2 * i)
            one(2 * i + 1)

    hops = list(range(2, last_even + 1, 2))
    near_hops, late_hops = hops[:len(hops) // 2], hops[len(hops) // 2:]

    def pass_all(which, h):
        for j in which:
            pass_on(j, h)

    def gathered(c):
        cross[c].wait_recv()
        relays[c].start()

    for load in loads:
        load.wait()
    project(0, [(0, 0, rows)])
    sideways.wait_recv()
    project(0, [(1, 0, rows)])
    forward(0, 0)
    for c in range(pieces // 2):
        gathered(c)
    for c in range(pieces // 2):
        relays[c].wait_recv()
    project(1, [(2, 0, batch), (3, 0, batch)])
    forward(0, 1)
    pass_all(hops, 0)
    odd_arrivals(0)
    for c in range(pieces // 2, pieces):
        if c == pieces // 2:
            fold(0, 0, opening=True)
        if c == pieces - 1:
            pass_all(near_hops, 1)
            fold(1, 0, opening=True)
        gathered(c)
    for c in range(pieces // 2, pieces):
        relays[c].wait_recv()
    project(2, [(2, batch, batch), (3, batch, batch)])
    forward(0, 2)
    pass_all(late_hops, 1)
    fold(3, 0, opening=True)
    pass_all(near_hops, 2)
    odd_arrivals(1)
    fold(2, 0, opening=True)
    pass_all(late_hops, 2)
    fold(3, 1)
    fold(2, 1)
    odd_arrivals(2)

    load_out.wait()
    wide = weight_out.shape[1] // chunks

    def share(block_of, c):
        first = pl.multiple_of(block_of * rows, rows)
        columns = pl.ds(pl.multiple_of(c * wide, wide), wide)
        joined = jnp.concatenate([attended[g, pl.ds(first, rows), :] for g in range(heads)], axis=1)
        return jnp.dot(joined, weight_out[:, columns], preferred_element_type=jnp.float32)

    def hand(src, dst, send, recv, c, other):
        return remote(src.at[c], dst.at[c], send.at[c], recv.at[c], "tensor", other)

    copy_a = lambda c: hand(part_a, got_a, send_a, recv_a, c, near)
    copy_b = lambda c: hand(part_b, got_b, send_b, recv_b, c, far)
    copy_c = lambda c: hand(part_c, got_c, send_c, recv_c, c, near)

    fold(3, 2, closing=True)

    @pl.loop(0, chunks)
    def _(c):
        part_a[c] = share(flip(me, 3), c).astype(jnp.bfloat16)
        copy_a(c).start()

    fold(2, 2, closing=True)

    @pl.loop(0, chunks)
    def _(c):
        own = share(far, c)
        copy_a(c).wait_recv()
        part_b[c] = (own + got_a[c].astype(jnp.float32)).astype(jnp.bfloat16)
        copy_b(c).start()

    fold(1, 1)
    fold(1, 2, closing=True)

    @pl.loop(0, chunks)
    def _(c):
        part_c[c] = share(near, c).astype(jnp.bfloat16)
        copy_c(c).start()

    fold(0, 1)
    fold(0, 2, closing=True)

    @pl.loop(0, chunks)
    def _(c):
        columns = pl.ds(pl.multiple_of(c * wide, wide), wide)
        result = share(me, c) + held[0, :, columns].astype(jnp.float32)
        copy_c(c).wait_recv()
        result = result + got_c[c].astype(jnp.float32)
        copy_b(c).wait_recv()
        out_ref[:, columns] = (result + got_b[c].astype(jnp.float32)).astype(jnp.bfloat16)

    @pl.loop(0, chunks)
    def _(c):
        copy_a(c).wait_send()
        copy_b(c).wait_send()
        copy_c(c).wait_send()

    sideways.wait_send()
    for copy in cross + relays:
        copy.wait_send()
    for h in range(3):
        for j in range(0, last_even + 1, 2):
            settle(j, h)


def body(tokens, norm_gain, w_query, key_weight, value_weight, w_out, lengths):
    dp = lax.axis_size("dp")
    rows, width = tokens.shape
    count = 4 * rows
    heads = w_query.shape[1] // HEAD_SIZE
    total = w_query.shape[1] + key_weight.shape[1] + value_weight.shape[1]
    reach = min(dp // 2 + 1, dp - 1)
    slots = reach + 1
    pieces, chunks = 4, 8
    exponent = jnp.arange(HEAD_SIZE // 2, dtype=jnp.float32) * (-2.0 / HEAD_SIZE)
    frequency = jnp.tile(rope_base**exponent, 2)[None, :]
    any_spec = pl.BlockSpec(memory_space=pl.ANY)
    vmem = pl.BlockSpec(memory_space=pltpu.VMEM)
    smem = pl.BlockSpec(memory_space=pltpu.SMEM)
    bf16, f32 = jnp.bfloat16, jnp.float32
    part = pltpu.VMEM((chunks, rows, width // chunks), bf16)
    dma = pltpu.SemaphoreType.DMA
    return pl.pallas_call(
        functools.partial(kernel, dp, reach, pieces, chunks),
        out_shape=jax.ShapeDtypeStruct((rows, width), bf16),
        in_specs=[smem, vmem, vmem, any_spec, any_spec, any_spec, any_spec, any_spec],
        out_specs=vmem,
        scratch_shapes=[
            pltpu.VMEM((4, rows, width), bf16),
            pltpu.VMEM((rows, width), bf16),
            pltpu.VMEM((width, total), bf16),
            pltpu.VMEM((rows, total), f32),
            pltpu.VMEM((count, HEAD_SIZE), f32),
            pltpu.VMEM((count, HEAD_SIZE), f32),
            pltpu.VMEM((heads, count, 2 * HEAD_SIZE), bf16),
            pltpu.VMEM((slots * 2 * rows, 3 * HEAD_SIZE), bf16),
            pltpu.VMEM((slots * rows, 3 * HEAD_SIZE), bf16),
            pltpu.VMEM((slots * rows, 3 * HEAD_SIZE), bf16),
            pltpu.VMEM((heads, count, 1), f32),
            pltpu.VMEM((heads, count, 1), f32),
            pltpu.VMEM((heads, count, HEAD_SIZE), f32),
            pltpu.VMEM((heads, count, HEAD_SIZE), bf16),
            pltpu.VMEM(w_out.shape, bf16),
            part, part, part, part, part, part,
            dma((5,)), dma, dma,
            dma((pieces,)), dma((pieces,)), dma((pieces,)), dma((pieces,)),
            dma((slots, 3)), dma((slots, 3)), dma((3,)), dma((slots, 3)),
            dma((chunks,)), dma((chunks,)), dma((chunks,)), dma((chunks,)), dma((chunks,)), dma((chunks,)),
        ],
        compiler_params=pltpu.CompilerParams(
            collective_id=0, has_side_effects=True, vmem_limit_bytes=62 * 2**20
        ),
        name="attention_block",
    )(lengths, norm_gain[None, :], frequency, tokens, w_query, key_weight, value_weight, w_out)


def solution(mesh):
    in_specs = (
        P(("dp", "tensor"), None),
        P(),
        P(None, "tensor"),
        P(None, "tensor"),
        P(None, "tensor"),
        P("tensor", None),
        P(),
    )
    out_specs = P(("dp", "tensor"), None)
    return jax.shard_map(body, mesh=mesh, in_specs=in_specs, out_specs=out_specs, check_vma=False)
```
